32 devices in a mesh: rows: 4 (over z), cent: 8 (over y, x, core).
Axes of the slice: x: 2, y: 2, z: 4, core: 2. Of those that a mesh axis runs over, the one named last changes fastest.
Arguments:
- train_rows: float32 [16384, 64], P('rows'), may hold values from -6 to 6
- centre_index: int32 [16384], P('cent'), may hold values from 0 to 16383
- precond: bfloat16 [16384, 16384], P('cent', 'rows'), as said below
- coefficients: float32 [16384, 128], P(('rows', 'cent')), may hold values from -6 to 6
- residual: float32 [16384, 128], P(('rows', 'cent')), may hold values from -6 to 6
- direction: float32 [16384, 128], P(('rows', 'cent')), may hold values from -6 to 6
Outputs:
- coef_next: float32 [16384, 128], P(('rows', 'cent'))
- residual_next: float32 [16384, 128], P(('rows', 'cent'))
- direction_next: float32 [16384, 128], P(('rows', 'cent'))
The draws below stay inside these ranges and needn't reach their ends.
Inputs may be any that keep to these rules, and one draw needn't show every extreme that they name: precond is zero below its diagonal.
All inputs are finite; a program needn't handle non-finite values.
Results may differ from the reference program's by a relative error of at most 0.0047.
Values may be sent and summed in bfloat16 or wider, within the bound.
A program may use at most 128 MiB of HBM per device.

```python
import math
import jax
import jax.numpy as jnp
from jax import lax

ROWS_DEV = 4096
CENTRES = 16384
FEAT = 64
OUTS = 128
TRAIN = 16384


def draw_precond(key, part):
    first, second = jax.random.split(jax.random.fold_in(key, 11))
    upper_part = jax.random.normal(first, (CENTRES, CENTRES), jnp.float32) * CENTRES ** (-0.5)
    diag_vals = jnp.exp(jax.random.uniform(second, (CENTRES,), jnp.float32, math.log(0.5), math.log(2.0)))
    row_ids = jnp.arange(CENTRES)[:, None]
    col_ids = jnp.arange(CENTRES)[None, :]
    matrix = jnp.where(col_ids > row_ids, upper_part, 0.0) + jnp.where(col_ids == row_ids, diag_vals[:, None], 0.0)
    return matrix.astype(jnp.bfloat16)


def draw_train_rows(key, part):
    subkeys = jax.random.split(jax.random.fold_in(key, 23), 4)
    groups = max(TRAIN // 64, 2)
    member = jax.random.randint(subkeys[0], (TRAIN,), 0, groups)
    cluster_mean = 1.2 * jax.random.normal(subkeys[1], (groups, FEAT), jnp.float32)
    spread = jnp.full((groups, 1), 0.5, jnp.float32)
    jitter = jax.random.normal(subkeys[3], (TRAIN, FEAT), jnp.float32)
    points = cluster_mean[member] + spread[member] * jitter
    return jnp.clip(points, -6.0, 6.0)


def plant(entries, own_key, least, top_value):
    spot = [jax.random.randint(jax.random.fold_in(own_key, axis), (), 0, length) for axis, length in enumerate(entries.shape)]
    longest = entries.shape.index(max(entries.shape))
    beside = spot[:longest] + [(spot[longest] + 1) % entries.shape[longest]] + spot[longest + 1:]
    return entries.at[tuple(spot)].set(least).at[tuple(beside)].set(top_value)


def levels(own_key, dims, cuts, low, high):
    def one(axis_at, blocks):
        heights = jax.random.uniform(jax.random.fold_in(jax.random.fold_in(own_key, 6), axis_at), (blocks,), jnp.float32, low / len(cuts), high / len(cuts))
        return jnp.repeat(jnp.exp(heights), dims[axis_at] // blocks).reshape((-1,) + (1,) * (len(dims) - axis_at - 1))

    gain = one(*cuts[0])
    for cut in cuts[1:]:
        gain = gain * one(*cut)
    return gain


def scatter_about(own_key, dims, deviation, most, shards=(), held_as=jnp.bfloat16):
    values = deviation * jax.random.normal(own_key, dims, jnp.float32)
    if shards:
        values = values * levels(own_key, dims, shards, -0.22, 0.18)
    return jnp.clip(values, -most, most).astype(held_as)


def setup_inputs(seed: int = 0) -> dict:
    key_of = jax.random.split(jax.random.key(seed), 7)
    return {
        "train_rows": draw_train_rows(jax.random.fold_in(key_of[6], 71), 0),
        "centre_index": plant(jax.random.randint(key_of[1], (CENTRES,), 0, TRAIN), jax.random.fold_in(key_of[1], 1), 0, TRAIN - 1).astype(jnp.int32),
        "precond": draw_precond(jax.random.fold_in(key_of[6], 71), 0),
        "coefficients": scatter_about(key_of[3], (CENTRES, OUTS), 1.0, 6.0, ((0, 32),), jnp.float32),
        "residual": scatter_about(key_of[4], (CENTRES, OUTS), 1.0, 6.0, ((0, 32),), jnp.float32),
        "direction": scatter_about(key_of[5], (CENTRES, OUTS), 1.0, 6.0, ((0, 32),), jnp.float32),
    }


ridge_weight = 0.1


def kernel_tile(block_rows, centres):
    row_sq = jnp.sum(block_rows * block_rows, axis=1)
    cen_sq = jnp.sum(centres * centres, axis=1)
    cross = jnp.dot(block_rows, centres.T, precision=lax.Precision.HIGHEST, preferred_element_type=jnp.float32)
    distance = row_sq[:, None] + cen_sq[None, :] - 2.0 * cross
    return jnp.exp(-(2.0 / FEAT) * distance).astype(jnp.bfloat16)


def reference(train_rows, centre_index, precond, coefficients, residual, direction):
    centres = train_rows[centre_index.astype(jnp.int32)]
    block_size = min(ROWS_DEV, 1024)
    row_blocks = train_rows.reshape(TRAIN // block_size, block_size, FEAT)
    dir_low = direction.astype(jnp.bfloat16)
    coef_field = jnp.dot(precond, dir_low, preferred_element_type=jnp.float32).astype(jnp.bfloat16)

    def forward(block_rows):
        return jnp.dot(kernel_tile(block_rows, centres), coef_field, preferred_element_type=jnp.float32).astype(jnp.bfloat16)

    fitted = lax.map(forward, row_blocks)

    def accumulate(total, pair):
        block_rows, fitted_block = pair
        tile = kernel_tile(block_rows, centres)
        return total + lax.dot_general(tile, fitted_block, (((0,), (0,)), ((), ())), preferred_element_type=jnp.float32), None

    grad, unused = lax.scan(accumulate, jnp.zeros((CENTRES, OUTS), jnp.float32), (row_blocks, fitted))
    grad_low = (grad * (float(TRAIN) ** -0.5)).astype(jnp.bfloat16)
    image = lax.dot_general(precond, grad_low, (((0,), (0,)), ((), ())), preferred_element_type=jnp.float32)
    image = image + ridge_weight * direction
    norm_old = jnp.sum(residual * residual)
    curvature = jnp.sum(direction * image)
    step_size = norm_old / curvature
    coef_next = coefficients + step_size * direction
    residual_next = residual - step_size * image
    norm_new = jnp.sum(residual_next * residual_next)
    direction_next = residual_next + (norm_new / norm_old) * direction
    return coef_next, residual_next, direction_next
```

```python
import functools
import math

import jax
import jax.numpy as jnp
from jax import lax
from jax.experimental import pallas as pl
from jax.experimental.pallas import tpu as pltpu
from jax.sharding import PartitionSpec as P

FEAT = 64
OUTS = 128
CHUNK = 256
GROUPS = 2
LAG = 4
COEF_AT = 10
BUILD_AFTER = 8
WIDEST = 6.0
F32 = jnp.float32
BF16 = jnp.bfloat16
I16 = jnp.int16
I32 = jnp.int32
MESH = pl.DeviceIdType.MESH
STEPS = 5461.0
LOG2E = math.log2(math.e)
CROSS = LOG2E * 4.0 / FEAT / STEPS
POINT_NORM = -STEPS * STEPS * FEAT / (8.0 * LOG2E)
CENTRE_NORM = -LOG2E * 2.0 / FEAT / (STEPS * STEPS)

ridge_weight = 0.1


def dot(a, b):
    return jnp.dot(a, b, preferred_element_type=F32)


def dot_t(a, b):
    return lax.dot_general(a, b, (((1,), (1,)), ((), ())), preferred_element_type=F32)


def three(value):
    high = value.astype(BF16)
    rest = value - high.astype(F32)
    middle = rest.astype(BF16)
    low = (rest - middle.astype(F32)).astype(BF16)
    return high.astype(F32), middle.astype(F32), low.astype(F32)


def augmented(high, low, norm_scale, norm_at, one_at):
    exact = high + low
    norm = norm_scale * jnp.sum(exact * exact, axis=0, keepdims=True)
    sub = lax.broadcasted_iota(I32, high.shape, 0)
    extra = jnp.where((sub >= one_at) & (sub < one_at + 3), 1.0, 0.0)
    for at, term in enumerate(three(norm)):
        extra = jnp.where(sub == norm_at + at, term, extra)
    return extra


def step_kernel(
    rows_n, cent_n,
    idx_ref, x_ref, p_hbm, res_ref, dir_ref,
    image_ref, sums_ref,
    p_buf, p_sem, kt_buf, xaug_t, nhl_t,
    pick, coef, grad,
    dir_own, dir_all, fit_own, fit_all, gather_sems,
    fit_acc, fit_rs, img_acc, img_rs,
    sc_own, sc_cent, sc_mid, sc_rows, sc_sems,
):
    z = lax.axis_index("rows")
    me = lax.axis_index("cent")
    core = lax.rem(me, 2)
    chip = lax.div(me, 2)
    other = chip * 2 + (1 - core)
    chips = cent_n // 2
    chunks = p_buf.shape[0]
    rows_here = x_ref.shape[1]
    part = dir_own.shape[1]
    fit_part = fit_acc.shape[3]
    group = OUTS // GROUPS
    items = GROUPS * chunks
    last = rows_n - 1
    reach = LAG * last

    def chip_at(distance):
        return lax.rem(chip + distance, chips)

    def p_copy(k):
        return pltpu.make_async_copy(
            p_hbm.at[pl.ds(pl.multiple_of(k * CHUNK, CHUNK), CHUNK)], p_buf.at[k], p_sem.at[k]
        )

    barrier = pltpu.get_barrier_semaphore()
    for d in range(1, cent_n):
        pl.semaphore_signal(
            barrier, inc=1, device_id=(z, lax.rem(me + d, cent_n)), device_id_type=MESH
        )
    for d in range(1, rows_n):
        pl.semaphore_signal(
            barrier, inc=1, device_id=(lax.rem(z + d, rows_n), me), device_id_type=MESH
        )

    @pl.loop(0, chunks)
    def _(k):
        p_copy(k).start()

    dir_own[...] = dir_ref[...].T.astype(BF16)
    for scan in (pick, coef, grad):
        @pl.when(z == 0)
        def _():
            scan[3][...] = jnp.zeros_like(scan[3])

        @pl.when(z == last)
        def _():
            scan[4][...] = jnp.zeros_like(scan[4])

    pl.semaphore_wait(barrier, cent_n - 1 + rows_n - 1)

    def gather_copy(which, own, whole, d):
        target = other if d == 0 else chip_at(d) * 2 + core
        return pltpu.make_async_remote_copy(
            src_ref=own, dst_ref=whole.at[me],
            send_sem=gather_sems.at[which, 0, d], recv_sem=gather_sems.at[which, 1, d],
            device_id=(z, target), device_id_type=MESH,
        )

    def forward_copy(which, whole, d):
        source = chip_at(chips - d) * 2 + core
        return pltpu.make_async_remote_copy(
            src_ref=whole.at[source], dst_ref=whole.at[source],
            send_sem=gather_sems.at[which, 2, d], recv_sem=gather_sems.at[which, 3, d],
            device_id=(z, other), device_id_type=MESH,
        )

    def gather_start(which, own, whole):
        for d in list(range(1, chips)) + [0]:
            gather_copy(which, own, whole, d).start()
        whole[me] = own[...]

    def gather_forward(which, own, whole):
        for d in range(1, chips):
            gather_copy(which, own, whole, d).wait_recv()
            forward_copy(which, whole, d).start()

    def gather_end(which, own, whole):
        gather_copy(which, own, whole, 0).wait_recv()
        for d in range(1, chips):
            forward_copy(which, whole, d).wait_recv()

    def gather_sent(which, own, whole):
        for d in range(chips):
            gather_copy(which, own, whole, d).wait_send()
        for d in range(1, chips):
            forward_copy(which, whole, d).wait_send()

    def right_copy(scan, k):
        own, to_right, to_left, from_left, from_right, sems = scan
        return pltpu.make_async_remote_copy(
            src_ref=to_right.at[k], dst_ref=from_left.at[k],
            send_sem=sems.at[0, k], recv_sem=sems.at[1, k],
            device_id=(lax.rem(z + 1, rows_n), me), device_id_type=MESH,
        )

    def left_copy(scan, k):
        own, to_right, to_left, from_left, from_right, sems = scan
        return pltpu.make_async_remote_copy(
            src_ref=to_left.at[k], dst_ref=from_right.at[k],
            send_sem=sems.at[2, k], recv_sem=sems.at[3, k],
            device_id=(lax.rem(z + last, rows_n), me), device_id_type=MESH,
        )

    def wide(scan):
        return I32 if scan[0].dtype == I16 else F32

    def scan_step(scan, it):
        own, to_right, to_left, from_left, from_right, sems = scan
        kr = it - LAG * z
        kl = it - LAG * (last - z)
        kind = wide(scan)

        @pl.when((kr >= 0) & (kr < own.shape[0]) & (z < last))
        def _():
            @pl.when(z > 0)
            def _():
                right_copy(scan, kr).wait_recv()

            to_right[kr] = (own[kr].astype(kind) + from_left[kr].astype(kind)).astype(to_right.dtype)
            right_copy(scan, kr).start()

        @pl.when((kl >= 0) & (kl < own.shape[0]) & (z > 0))
        def _():
            @pl.when(z < last)
            def _():
                left_copy(scan, kl).wait_recv()

            to_left[kl] = (own[kl].astype(kind) + from_right[kl].astype(kind)).astype(to_left.dtype)
            left_copy(scan, kl).start()

    def scan_total(scan, k):
        own, to_right, to_left, from_left, from_right, sems = scan
        kind = wide(scan)

        @pl.when(z == last)
        def _():
            right_copy(scan, k).wait_recv()

        @pl.when(z == 0)
        def _():
            left_copy(scan, k).wait_recv()

        return own[k].astype(kind) + from_left[k].astype(kind) + from_right[k].astype(kind)

    def scan_sent(scan):
        @pl.loop(0, scan[0].shape[0])
        def _(k):
            @pl.when(z < last)
            def _():
                right_copy(scan, k).wait_send()

            @pl.when(z > 0)
            def _():
                left_copy(scan, k).wait_send()

    def across_copy(buffers, g, q):
        send_a, recv_a, send_b, recv_b, sems = buffers
        return pltpu.make_async_remote_copy(
            src_ref=send_a.at[g, q], dst_ref=recv_a.at[g, q],
            send_sem=sems.at[g, 0, q], recv_sem=sems.at[g, 1, q],
            device_id=(z, other), device_id_type=MESH,
        )

    def between_copy(buffers, g, d):
        send_a, recv_a, send_b, recv_b, sems = buffers
        return pltpu.make_async_remote_copy(
            src_ref=send_b.at[g, d], dst_ref=recv_b.at[g, d],
            send_sem=sems.at[g, 2, d], recv_sem=sems.at[g, 3, d],
            device_id=(z, chip_at(d) * 2 + core), device_id_type=MESH,
        )

    def scatter_across(acc, buffers, g):
        for d in list(range(1, chips)) + [0]:
            q = chip_at(d)
            buffers[0][g, q] = acc[g, q * 2 + (1 - core)].astype(BF16)
            across_copy(buffers, g, q).start()

    def scatter_between(acc, buffers, g):
        send_a, recv_a, send_b, recv_b, sems = buffers
        for d in range(1, chips):
            q = chip_at(d)
            across_copy(buffers, g, q).wait_recv()
            send_b[g, d] = (acc[g, q * 2 + core] + recv_a[g, q].astype(F32)).astype(BF16)
            between_copy(buffers, g, d).start()

    def scatter_end(acc, buffers, g):
        send_a, recv_a, send_b, recv_b, sems = buffers
        across_copy(buffers, g, chip).wait_recv()
        total = acc[g, me] + recv_a[g, chip].astype(F32)
        for d in range(1, chips):
            between_copy(buffers, g, d).wait_recv()
            total = total + recv_b[g, d].astype(F32)
        return total

    def scatter_sent(buffers):
        for g in range(GROUPS):
            for d in range(chips):
                across_copy(buffers, g, chip_at(d)).wait_send()
            for d in range(1, chips):
                between_copy(buffers, g, d).wait_send()

    gather_start(0, dir_own, dir_all)

    x_block = rows_here // chunks
    for b in range(chunks):
        here = slice(b * x_block, (b + 1) * x_block)
        number = jnp.round(x_ref[:, here] * STEPS)
        high = number.astype(BF16)
        nhl_t[:FEAT, here] = high
        nhl_t[FEAT:, here] = (number - high.astype(F32)).astype(BF16)

    def augment_points(b):
        here = pl.ds(pl.multiple_of(b * x_block, x_block), x_block)
        points = x_ref[:, here] * CROSS
        high = points.astype(BF16).astype(F32)
        low = (points - high).astype(BF16).astype(F32)
        extra = augmented(high, low, POINT_NORM, 0, 3)
        for at, term in enumerate((high, low, high, extra)):
            xaug_t[at * FEAT : (at + 1) * FEAT, here] = term.astype(BF16)

    pick_block = math.gcd(rows_here, 1024)

    def pick_own(k):
        wanted = idx_ref[k] - z * rows_here
        total = jnp.zeros((2 * FEAT, CHUNK), F32)
        for b in range(rows_here // pick_block):
            ids = lax.broadcasted_iota(I32, (pick_block, CHUNK), 0) + b * pick_block
            hot = jnp.where(ids == wanted, 1.0, 0.0).astype(BF16)
            total = total + dot(nhl_t[:, b * pick_block : (b + 1) * pick_block], hot)
        pick[0][k] = (total[:FEAT] + total[FEAT:]).astype(I32).astype(I16)

    def coef_own(k):
        p_copy(k).wait()
        total = jnp.zeros((OUTS, CHUNK), F32)
        for b in range(cent_n):
            total = total + dot_t(dir_all[b], p_buf[k, :, b * part : (b + 1) * part])
        for g in range(GROUPS):
            coef[0][g * chunks + k] = total[g * group : (g + 1) * group]

    k_block = math.gcd(rows_here, 512)

    def build(k):
        number = scan_total(pick, k).astype(F32)
        high = number.astype(BF16).astype(F32)
        low = number - high
        extra = augmented(high, low, CENTRE_NORM, 3, 0)
        caug = jnp.concatenate([high, high, low, extra], axis=0).T.astype(BF16)
        for b in range(rows_here // k_block):
            here = slice(b * k_block, (b + 1) * k_block)
            kt_buf[k, :, here] = jnp.exp2(dot(caug, xaug_t[:, here])).astype(BF16)

    def fit_add(i):
        g = lax.div(i, chunks)
        k = lax.rem(i, chunks)
        low = scan_total(coef, i).astype(BF16)
        for b in range(cent_n):
            fit_acc[g, b] += dot(low, kt_buf[k, :, b * fit_part : (b + 1) * fit_part])

    fit_acc[...] = jnp.zeros_like(fit_acc)
    img_acc[...] = jnp.zeros_like(img_acc)
    build_at = COEF_AT + BUILD_AFTER
    fit_at = COEF_AT + reach

    @pl.loop(0, fit_at + items)
    def _(it):
        @pl.when(it < chunks)
        def _():
            pick_own(it)

        scan_step(pick, it)

        @pl.when(it < chunks)
        def _():
            augment_points(it)

        @pl.when(it == COEF_AT)
        def _():
            gather_forward(0, dir_own, dir_all)
            gather_end(0, dir_own, dir_all)

        @pl.when((it >= COEF_AT) & (it < COEF_AT + chunks))
        def _():
            coef_own(it - COEF_AT)

        scan_step(coef, it - COEF_AT)

        @pl.when((it >= build_at) & (it < build_at + chunks))
        def _():
            build(it - build_at)

        @pl.when(it >= fit_at)
        def _():
            fit_add(it - fit_at)

        for g in range(GROUPS):
            done = fit_at + (g + 1) * chunks - 1

            @pl.when(it == done)
            def _():
                scatter_across(fit_acc, fit_rs, g)

            if g < GROUPS - 1:
                @pl.when(it == done + 2)
                def _():
                    scatter_between(fit_acc, fit_rs, g)

    def fit_shared(g):
        fit_own[g] = scatter_end(fit_acc, fit_rs, g).astype(BF16)
        gather_start(1 + g, fit_own.at[g], fit_all.at[g])

    for g in range(GROUPS - 1):
        fit_shared(g)
    scatter_between(fit_acc, fit_rs, GROUPS - 1)
    for g in range(GROUPS - 1):
        gather_forward(1 + g, fit_own.at[g], fit_all.at[g])
    fit_shared(GROUPS - 1)
    gather_end(1, fit_own.at[0], fit_all.at[0])

    scale = float(rows_here * rows_n) ** -0.5

    def grad_own(i):
        g = lax.div(i, chunks)
        k = lax.rem(i, chunks)
        total = jnp.zeros((group, CHUNK), F32)
        for b in range(cent_n):
            total = total + dot_t(fit_all[g, b], kt_buf[k, :, b * fit_part : (b + 1) * fit_part])
        grad[0][i] = total

    def img_add(i):
        g = lax.div(i, chunks)
        k = lax.rem(i, chunks)
        low = (scan_total(grad, i) * scale).astype(BF16)
        for b in range(cent_n):
            img_acc[g, b] += dot(low, p_buf[k, :, b * part : (b + 1) * part])

    @pl.loop(0, items + reach)
    def _(it):
        for g in range(1, GROUPS):
            @pl.when(it == g * chunks)
            def _():
                if g == GROUPS - 1:
                    gather_forward(1 + g, fit_own.at[g], fit_all.at[g])
                gather_end(1 + g, fit_own.at[g], fit_all.at[g])

        @pl.when(it < items)
        def _():
            grad_own(it)

        scan_step(grad, it)

        @pl.when(it >= reach)
        def _():
            img_add(it - reach)

        for g in range(GROUPS):
            done = reach + (g + 1) * chunks - 1

            @pl.when(it == done)
            def _():
                scatter_across(img_acc, img_rs, g)

            if g < GROUPS - 1:
                @pl.when(it == done + 2)
                def _():
                    scatter_between(img_acc, img_rs, g)

    images = [scatter_end(img_acc, img_rs, g) for g in range(GROUPS - 1)]
    scatter_between(img_acc, img_rs, GROUPS - 1)
    images.append(scatter_end(img_acc, img_rs, GROUPS - 1))
    image = jnp.concatenate(images, axis=0).T
    image = image + ridge_weight * dir_ref[...]
    image_ref[...] = image

    def rows_sum(value):
        return jnp.sum(value, axis=0, keepdims=True)

    residual = res_ref[...]
    sc_own[...] = jnp.concatenate(
        [
            rows_sum(residual * residual),
            rows_sum(dir_ref[...] * image),
            rows_sum(residual * image),
            rows_sum(image * image),
            jnp.zeros((4, OUTS), F32),
        ],
        axis=0,
    )

    def cent_copy(d):
        return pltpu.make_async_remote_copy(
            src_ref=sc_own, dst_ref=sc_cent.at[d],
            send_sem=sc_sems.at[0, d], recv_sem=sc_sems.at[1, d],
            device_id=(z, lax.rem(me + d, cent_n)), device_id_type=MESH,
        )

    def rows_copy(d):
        return pltpu.make_async_remote_copy(
            src_ref=sc_mid, dst_ref=sc_rows.at[d],
            send_sem=sc_sems.at[2, d], recv_sem=sc_sems.at[3, d],
            device_id=(lax.rem(z + d, rows_n), me), device_id_type=MESH,
        )

    for d in range(1, cent_n):
        cent_copy(d).start()
    total = sc_own[...]
    for d in range(1, cent_n):
        cent_copy(d).wait_recv()
        total = total + sc_cent[d]
    sc_mid[...] = total
    for d in range(1, rows_n):
        rows_copy(d).start()
    gather_sent(0, dir_own, dir_all)
    for g in range(GROUPS):
        gather_sent(1 + g, fit_own.at[g], fit_all.at[g])
    scatter_sent(fit_rs)
    scatter_sent(img_rs)
    scan_sent(pick)
    scan_sent(coef)
    scan_sent(grad)
    for d in range(1, cent_n):
        cent_copy(d).wait_send()
    for d in range(1, rows_n):
        rows_copy(d).wait_recv()
        total = total + sc_rows[d]
    sums_ref[...] = total
    for d in range(1, rows_n):
        rows_copy(d).wait_send()


def update_kernel(sums_ref, image_ref, coef_ref, res_ref, dir_ref, coef_out, res_out, dir_out):
    totals = jnp.sum(sums_ref[...], axis=1, keepdims=True)
    norm_old, curvature, cross, square = (totals[at : at + 1] for at in range(4))
    step_size = norm_old / curvature
    norm_new = norm_old - 2.0 * step_size * cross + step_size * step_size * square
    ratio = norm_new / norm_old
    direction = dir_ref[...]
    coef_out[...] = coef_ref[...] + step_size * direction
    residual_next = res_ref[...] - step_size * image_ref[...]
    res_out[...] = residual_next
    dir_out[...] = residual_next + ratio * direction


def on_device(rows_n, cent_n, train_rows, centre_index, precond, coefficients, residual, direction):
    rows_here = train_rows.shape[0]
    centres_here = centre_index.shape[0]
    part = direction.shape[0]
    chunks = centres_here // CHUNK
    chips = cent_n // 2
    fit_part = rows_here // cent_n
    group = OUTS // GROUPS
    vmem = pl.BlockSpec(memory_space=pltpu.VMEM)

    def scan(count, shape, own_dtype, link_dtype):
        piece = (count,) + shape
        return (
            pltpu.VMEM(piece, own_dtype),
            pltpu.VMEM(piece, link_dtype), pltpu.VMEM(piece, link_dtype),
            pltpu.VMEM(piece, link_dtype), pltpu.VMEM(piece, link_dtype),
            pltpu.SemaphoreType.DMA((4, count)),
        )

    def scatter(shape):
        piece = (GROUPS, chips) + shape
        return (
            pltpu.VMEM(piece, BF16), pltpu.VMEM(piece, BF16),
            pltpu.VMEM(piece, BF16), pltpu.VMEM(piece, BF16),
            pltpu.SemaphoreType.DMA((GROUPS, 4, chips)),
        )

    image, sums = pl.pallas_call(
        functools.partial(step_kernel, rows_n, cent_n),
        out_shape=(
            jax.ShapeDtypeStruct((part, OUTS), F32),
            jax.ShapeDtypeStruct((8, OUTS), F32),
        ),
        in_specs=[vmem, vmem, pl.BlockSpec(memory_space=pl.ANY), vmem, vmem],
        out_specs=(vmem, vmem),
        scratch_shapes=[
            pltpu.VMEM((chunks, CHUNK, precond.shape[1]), BF16),
            pltpu.SemaphoreType.DMA((chunks,)),
            pltpu.VMEM((chunks, CHUNK, rows_here), BF16),
            pltpu.VMEM((4 * FEAT, rows_here), BF16),
            pltpu.VMEM((2 * FEAT, rows_here), BF16),
            scan(chunks, (FEAT, CHUNK), I16, I16),
            scan(GROUPS * chunks, (group, CHUNK), F32, BF16),
            scan(GROUPS * chunks, (group, CHUNK), F32, BF16),
            pltpu.VMEM((OUTS, part), BF16),
            pltpu.VMEM((cent_n, OUTS, part), BF16),
            pltpu.VMEM((GROUPS, group, fit_part), BF16),
            pltpu.VMEM((GROUPS, cent_n, group, fit_part), BF16),
            pltpu.SemaphoreType.DMA((1 + GROUPS, 4, chips)),
            pltpu.VMEM((GROUPS, cent_n, group, fit_part), F32),
            scatter((group, fit_part)),
            pltpu.VMEM((GROUPS, cent_n, group, part), F32),
            scatter((group, part)),
            pltpu.VMEM((8, OUTS), F32),
            pltpu.VMEM((cent_n, 8, OUTS), F32),
            pltpu.VMEM((8, OUTS), F32),
            pltpu.VMEM((rows_n, 8, OUTS), F32),
            pltpu.SemaphoreType.DMA((4, max(cent_n, rows_n))),
        ],
        compiler_params=pltpu.CompilerParams(
            collective_id=0, has_side_effects=True, vmem_limit_bytes=67000000
        ),
        name="falkon_step",
    )(centre_index.reshape(chunks, 1, CHUNK), train_rows.T, precond, residual, direction)

    piece = jax.ShapeDtypeStruct((part, OUTS), F32)
    return pl.pallas_call(
        update_kernel,
        out_shape=(piece, piece, piece),
        in_specs=[vmem] * 5,
        out_specs=(vmem, vmem, vmem),
        name="falkon_update",
    )(sums, image, coefficients, residual, direction)


def solution(mesh):
    both = P(("rows", "cent"), None)
    return jax.shard_map(
        functools.partial(on_device, mesh.shape["rows"], mesh.shape["cent"]),
        mesh=mesh,
        in_specs=(P("rows", None), P("cent"), P("cent", "rows"), both, both, both),
        out_specs=(both, both, both),
        check_vma=False,
    )
```

```python
import functools
import math

import jax
import jax.numpy as jnp
from jax import lax
from jax.experimental import pallas as pl
from jax.experimental.pallas import tpu as pltpu
from jax.sharding import PartitionSpec as P

FEAT = 64
OUTS = 128
CHUNK = 256
GROUPS = 2
LAG = 5
CUTS = (1, 5, 7)
NEAR_AT = 8
NEAR_SLOTS = 4
FORWARD_BEFORE = 2
COEF_AT = 12
BUILD_AFTER = 0
WIDEST = 6.0
F32 = jnp.float32
BF16 = jnp.bfloat16
I16 = jnp.int16
I32 = jnp.int32
MESH = pl.DeviceIdType.MESH
STEPS = 5461.0
LOG2E = math.log2(math.e)
CROSS = LOG2E * 4.0 / FEAT / STEPS
POINT_NORM = -STEPS * STEPS * FEAT / (8.0 * LOG2E)
CENTRE_NORM = -LOG2E * 2.0 / FEAT / (STEPS * STEPS)

ridge_weight = 0.1


def dot(a, b):
    return jnp.dot(a, b, preferred_element_type=F32)


def dot_t(a, b):
    return lax.dot_general(a, b, (((1,), (1,)), ((), ())), preferred_element_type=F32)


def three(value):
    high = value.astype(BF16)
    rest = value - high.astype(F32)
    middle = rest.astype(BF16)
    low = (rest - middle.astype(F32)).astype(BF16)
    return high.astype(F32), middle.astype(F32), low.astype(F32)


def augmented(high, low, norm_scale, norm_at, one_at):
    exact = high + low
    norm = norm_scale * jnp.sum(exact * exact, axis=0, keepdims=True)
    sub = lax.broadcasted_iota(I32, high.shape, 0)
    extra = jnp.where((sub >= one_at) & (sub < one_at + 3), 1.0, 0.0)
    for at, term in enumerate(three(norm)):
        extra = jnp.where(sub == norm_at + at, term, extra)
    return extra


def step_kernel(
    rows_n, cent_n,
    idx_hbm, x_hbm, p_hbm, res_hbm, dir_hbm,
    image_ref, sums_ref,
    idx_ref, x_ref, res_ref, dir_ref, in_sems,
    p_buf, p_sem, k_buf, xaug, xaug_t, caug_t, nhl_t,
    pick, coef, grad,
    dir_own, dir_all, fit_own, fit_all, gather_sems,
    fit_acc, fit_rs, img_acc, img_rs,
    sc_own, sc_cent, sc_mid, sc_rows, sc_sems,
):
    z = lax.axis_index("rows")
    me = lax.axis_index("cent")
    core = lax.rem(me, 2)
    chip = lax.div(me, 2)
    other = chip * 2 + (1 - core)
    chips = cent_n // 2
    chunks = p_buf.shape[0]
    rows_here = x_ref.shape[1]
    part = dir_own.shape[1]
    fit_part = fit_acc.shape[2]
    group = OUTS // GROUPS
    items = GROUPS * chunks
    last = rows_n - 1
    reach = LAG * last

    near = chips - 1
    paired = chips & (chips - 1) == 0

    def chip_at(distance):
        if not paired:
            return lax.rem(chip + distance, chips)
        at = chip
        bit = 1
        while bit < chips:
            if distance & bit:
                at = at + bit * (1 - 2 * lax.rem(lax.div(at, bit), 2))
            bit *= 2
        return at

    def chip_from(distance):
        return chip_at(distance) if paired else chip_at(chips - distance)

    def p_copy(k):
        return pltpu.make_async_copy(
            p_hbm.at[pl.ds(pl.multiple_of(k * CHUNK, CHUNK), CHUNK)], p_buf.at[k], p_sem.at[k]
        )

    barrier = pltpu.get_barrier_semaphore()
    for d in range(1, cent_n):
        pl.semaphore_signal(
            barrier, inc=1, device_id=(z, lax.rem(me + d, cent_n)), device_id_type=MESH
        )
    for d in range(1, rows_n):
        pl.semaphore_signal(
            barrier, inc=1, device_id=(lax.rem(z + d, rows_n), me), device_id_type=MESH
        )

    inputs = [
        pltpu.make_async_copy(source, target, in_sems.at[at])
        for at, (source, target) in enumerate(
            ((dir_hbm, dir_ref), (x_hbm, x_ref), (idx_hbm, idx_ref), (res_hbm, res_ref))
        )
    ]
    for copy in inputs:
        copy.start()

    @pl.loop(0, chunks)
    def _(k):
        p_copy(k).start()

    inputs[0].wait()
    dir_own[...] = dir_ref[...].T.astype(BF16)
    for scan in (pick, coef, grad):
        @pl.when(z == 0)
        def _():
            scan[3][...] = jnp.zeros_like(scan[3])

        @pl.when(z == last)
        def _():
            scan[4][...] = jnp.zeros_like(scan[4])

    pl.semaphore_wait(barrier, cent_n - 1 + rows_n - 1)

    def gather_copy(which, own, whole, d):
        target = other if d == 0 else chip_at(d) * 2 + core
        return pltpu.make_async_remote_copy(
            src_ref=own, dst_ref=whole.at[me],
            send_sem=gather_sems.at[which, 0, d], recv_sem=gather_sems.at[which, 1, d],
            device_id=(z, target), device_id_type=MESH,
        )

    def forward_copy(which, whole, d):
        source = chip_from(d) * 2 + core
        return pltpu.make_async_remote_copy(
            src_ref=whole.at[source], dst_ref=whole.at[source],
            send_sem=gather_sems.at[which, 2, d], recv_sem=gather_sems.at[which, 3, d],
            device_id=(z, other), device_id_type=MESH,
        )

    def gather_start(which, own, whole):
        for d in list(range(1, chips)) + [0]:
            gather_copy(which, own, whole, d).start()
        whole[me] = own[...]

    def gather_forward(which, own, whole, distances):
        for d in distances:
            gather_copy(which, own, whole, d).wait_recv()
            forward_copy(which, whole, d).start()

    def gather_end(which, own, whole, distances):
        for d in distances:
            if d == 0:
                gather_copy(which, own, whole, 0).wait_recv()
            else:
                forward_copy(which, whole, d).wait_recv()

    def gather_sent(which, own, whole):
        for d in range(chips):
            gather_copy(which, own, whole, d).wait_send()
        for d in range(1, chips):
            forward_copy(which, whole, d).wait_send()

    def right_copy(scan, k):
        own, to_right, to_left, from_left, from_right, sems = scan
        return pltpu.make_async_remote_copy(
            src_ref=to_right.at[k], dst_ref=from_left.at[k],
            send_sem=sems.at[0, k], recv_sem=sems.at[1, k],
            device_id=(lax.rem(z + 1, rows_n), me), device_id_type=MESH,
        )

    def left_copy(scan, k):
        own, to_right, to_left, from_left, from_right, sems = scan
        return pltpu.make_async_remote_copy(
            src_ref=to_left.at[k], dst_ref=from_right.at[k],
            send_sem=sems.at[2, k], recv_sem=sems.at[3, k],
            device_id=(lax.rem(z + last, rows_n), me), device_id_type=MESH,
        )

    def wide(scan):
        return I32 if scan[0].dtype == I16 else F32

    def scan_step(scan, it):
        own, to_right, to_left, from_left, from_right, sems = scan
        kr = it - LAG * z
        kl = it - LAG * (last - z)
        kind = wide(scan)

        @pl.when((kr >= 0) & (kr < own.shape[0]) & (z < last))
        def _():
            @pl.when(z > 0)
            def _():
                right_copy(scan, kr).wait_recv()

            to_right[kr] = (own[kr].astype(kind) + from_left[kr].astype(kind)).astype(to_right.dtype)
            right_copy(scan, kr).start()

        @pl.when((kl >= 0) & (kl < own.shape[0]) & (z > 0))
        def _():
            @pl.when(z < last)
            def _():
                left_copy(scan, kl).wait_recv()

            to_left[kl] = (own[kl].astype(kind) + from_right[kl].astype(kind)).astype(to_left.dtype)
            left_copy(scan, kl).start()

    def scan_total(scan, k):
        own, to_right, to_left, from_left, from_right, sems = scan
        kind = wide(scan)

        @pl.when(z == last)
        def _():
            right_copy(scan, k).wait_recv()

        @pl.when(z == 0)
        def _():
            left_copy(scan, k).wait_recv()

        return own[k].astype(kind) + from_left[k].astype(kind) + from_right[k].astype(kind)

    def scan_sent(scan):
        @pl.loop(0, scan[0].shape[0])
        def _(k):
            @pl.when(z < last)
            def _():
                right_copy(scan, k).wait_send()

            @pl.when(z > 0)
            def _():
                left_copy(scan, k).wait_send()

    def across_copy(buffers, g, q):
        send_a, recv_a, send_b, recv_b, sems = buffers
        return pltpu.make_async_remote_copy(
            src_ref=send_a.at[g, q], dst_ref=recv_a.at[g, q],
            send_sem=sems.at[g, 0, q], recv_sem=sems.at[g, 1, q],
            device_id=(z, other), device_id_type=MESH,
        )

    def between_copy(buffers, g, d):
        send_a, recv_a, send_b, recv_b, sems = buffers
        return pltpu.make_async_remote_copy(
            src_ref=send_b.at[g, d], dst_ref=recv_b.at[g, d],
            send_sem=sems.at[g, 2, d], recv_sem=sems.at[g, 3, d],
            device_id=(z, chip_at(d) * 2 + core), device_id_type=MESH,
        )

    def scatter_across(mine, buffers, g):
        for d in list(range(1, chips)) + [0]:
            q = chip_at(d)
            buffers[0][g, q] = mine(g, q * 2 + (1 - core)).astype(BF16)
            across_copy(buffers, g, q).start()

    def scatter_between(mine, buffers, g):
        send_a, recv_a, send_b, recv_b, sems = buffers
        for d in range(1, chips):
            q = chip_at(d)
            across_copy(buffers, g, q).wait_recv()
            send_b[g, d] = (mine(g, q * 2 + core) + recv_a[g, q].astype(F32)).astype(BF16)
            between_copy(buffers, g, d).start()

    def scatter_end(mine, buffers, g):
        send_a, recv_a, send_b, recv_b, sems = buffers
        across_copy(buffers, g, chip).wait_recv()
        total = mine(g, me) + recv_a[g, chip].astype(F32)
        for d in range(1, chips):
            between_copy(buffers, g, d).wait_recv()
            total = total + recv_b[g, d].astype(F32)
        return total

    def scatter_sent(buffers):
        for g in range(GROUPS):
            for d in range(chips):
                across_copy(buffers, g, chip_at(d)).wait_send()
            for d in range(1, chips):
                between_copy(buffers, g, d).wait_send()

    gather_start(0, dir_own, dir_all)
    inputs[1].wait()
    inputs[2].wait()
    closer, farthest, every = range(1, near), range(near, chips), range(chips)

    x_block = rows_here // chunks
    for b in range(chunks):
        here = slice(b * x_block, (b + 1) * x_block)
        number = jnp.round(x_ref[:, here] * STEPS)
        high = number.astype(BF16)
        nhl_t[:FEAT, here] = high
        nhl_t[FEAT:, here] = (number - high.astype(F32)).astype(BF16)

    def augment_points(b):
        here = pl.ds(pl.multiple_of(b * x_block, x_block), x_block)
        points = x_ref[:, here] * CROSS
        high = points.astype(BF16).astype(F32)
        low = (points - high).astype(BF16).astype(F32)
        extra = augmented(high, low, POINT_NORM, 0, 3)
        for at, term in enumerate((high, low, high, extra)):
            xaug_t[at * FEAT : (at + 1) * FEAT, here] = term.astype(BF16)
        xaug[here, :] = jnp.concatenate([high, low, high, extra], axis=0).T.astype(BF16)

    pick_block = math.gcd(rows_here, 1024)

    def pick_own(k):
        wanted = idx_ref[k] - z * rows_here
        total = jnp.zeros((2 * FEAT, CHUNK), F32)
        for b in range(rows_here // pick_block):
            ids = lax.broadcasted_iota(I32, (pick_block, CHUNK), 0) + b * pick_block
            hot = jnp.where(ids == wanted, 1.0, 0.0).astype(BF16)
            total = total + dot(nhl_t[:, b * pick_block : (b + 1) * pick_block], hot)
        pick[0][k] = (total[:FEAT] + total[FEAT:]).astype(I32).astype(I16)

    def coef_blocks(k, blocks):
        total = jnp.zeros((OUTS, CHUNK), F32)
        for block in blocks:
            here = pl.ds(pl.multiple_of(block * part, part), part)
            total = total + dot_t(dir_all[block], p_buf[k, :, here])
        return total

    def pair(d):
        return [chip_from(d) * 2 + core, chip_from(d) * 2 + 1 - core]

    def coef_near(k):
        p_copy(k).wait()
        total = coef_blocks(k, [me, other] + [b for d in closer for b in pair(d)])
        for g in range(GROUPS):
            coef[0][k * GROUPS + g] = total[g * group : (g + 1) * group]

    def coef_far(k):
        total = coef_blocks(k, [b for d in farthest for b in pair(d)])
        for g in range(GROUPS):
            coef[0][k * GROUPS + g] += total[g * group : (g + 1) * group]

    fit_blocks = fit_part // CHUNK

    def build(k):
        number = scan_total(pick, k).astype(F32)
        high = number.astype(BF16).astype(F32)
        low = number - high
        extra = augmented(high, low, CENTRE_NORM, 3, 0)
        caug = jnp.concatenate([high, high, low, extra], axis=0)
        caug_t[k] = caug.astype(BF16)
        caug = caug.T.astype(BF16)
        for b in range(rows_here // CHUNK):
            here = slice(b * CHUNK, (b + 1) * CHUNK)
            k_buf[k, b] = jnp.exp2(dot(caug, xaug_t[:, here])).astype(BF16)

    def rebuild(k):
        for b in range(rows_here // CHUNK):
            here = slice(b * CHUNK, (b + 1) * CHUNK)
            k_buf[k, b] = jnp.exp2(dot(xaug[here, :], caug_t[k])).astype(BF16)

    def fit_add(k):
        low = jnp.concatenate(
            [scan_total(coef, k * GROUPS + g).astype(BF16) for g in range(GROUPS)], axis=0
        )
        for b in range(cent_n):
            for h in range(fit_blocks):
                here = slice(h * CHUNK, (h + 1) * CHUNK)
                fit_acc[b, :, here] += dot(low, k_buf[k, b * fit_blocks + h])

    def fit_mine(g, block):
        return fit_acc[block, g * group : (g + 1) * group, :]

    def img_mine(g, block):
        return img_acc[g, block]

    fit_acc[...] = jnp.zeros_like(fit_acc)
    img_acc[...] = jnp.zeros_like(img_acc)
    build_at = max(COEF_AT + BUILD_AFTER, LAG * (last - 1))
    fit_at = COEF_AT + reach

    def turn(it, start, phase):
        step = it - start
        return (step >= 0) & (step < items) & (lax.rem(step + items, GROUPS) == phase)

    @pl.loop(0, fit_at + items)
    def _(it):
        @pl.when(it < chunks)
        def _():
            pick_own(it)

        scan_step(pick, it)

        @pl.when(it < chunks)
        def _():
            augment_points(it)

        for at, distances in ((NEAR_AT, closer), (COEF_AT, farthest)):
            @pl.when(it == at - FORWARD_BEFORE)
            def _():
                gather_forward(0, dir_own, dir_all, distances)

            @pl.when(it == at)
            def _():
                if at == NEAR_AT:
                    gather_end(0, dir_own, dir_all, [0])
                gather_end(0, dir_own, dir_all, distances)

        @pl.when((it >= NEAR_AT) & (it < NEAR_AT + NEAR_SLOTS))
        def _():
            @pl.loop(0, chunks // NEAR_SLOTS)
            def _(step):
                coef_near((it - NEAR_AT) * (chunks // NEAR_SLOTS) + step)

        @pl.when(turn(it, COEF_AT, 0))
        def _():
            coef_far(lax.div(it - COEF_AT, GROUPS))

        scan_step(coef, it - COEF_AT)

        @pl.when(turn(it, build_at, GROUPS - 1))
        def _():
            build(lax.div(it - build_at, GROUPS))

        @pl.when(turn(it, fit_at, GROUPS - 1))
        def _():
            fit_add(lax.div(it - fit_at, GROUPS))

    def fit_shared(g):
        fit_own[g] = scatter_end(fit_mine, fit_rs, g).astype(BF16)
        gather_start(1 + g, fit_own.at[g], fit_all.at[g])

    def rebuild_some(start, stop):
        @pl.loop(start, stop)
        def _(k):
            rebuild(k)

    cuts = [chunks * c // 8 for c in CUTS]
    for g in range(GROUPS):
        scatter_across(fit_mine, fit_rs, g)
    rebuild_some(0, cuts[0])
    for g in range(GROUPS):
        scatter_between(fit_mine, fit_rs, g)
    rebuild_some(cuts[0], cuts[1])
    fit_shared(0)
    rebuild_some(cuts[1], cuts[2])
    for g in range(1, GROUPS):
        fit_shared(g)
    rebuild_some(cuts[2], chunks)
    gather_forward(1, fit_own.at[0], fit_all.at[0], range(1, chips))
    gather_end(1, fit_own.at[0], fit_all.at[0], every)

    scale = float(rows_here * rows_n) ** -0.5

    def grad_own(i):
        g = lax.div(i, chunks)
        k = lax.rem(i, chunks)
        total = jnp.zeros((group, CHUNK), F32)
        for b in range(cent_n):
            for h in range(fit_blocks):
                here = slice(h * CHUNK, (h + 1) * CHUNK)
                total = total + dot(fit_all[g, b, :, here], k_buf[k, b * fit_blocks + h])
        grad[0][i] = total

    def img_add(i):
        g = lax.div(i, chunks)
        k = lax.rem(i, chunks)
        low = (scan_total(grad, i) * scale).astype(BF16)
        for b in range(cent_n):
            img_acc[g, b] += dot(low, p_buf[k, :, b * part : (b + 1) * part])

    @pl.loop(0, items + reach)
    def _(it):
        @pl.when(it == (GROUPS - 1) * chunks - FORWARD_BEFORE)
        def _():
            g = GROUPS - 1
            gather_forward(1 + g, fit_own.at[g], fit_all.at[g], range(1, chips))

        for g in range(1, GROUPS):
            @pl.when(it == g * chunks)
            def _():
                gather_end(1 + g, fit_own.at[g], fit_all.at[g], every)

        @pl.when(it < items)
        def _():
            grad_own(it)

        scan_step(grad, it)

        @pl.when(it >= reach)
        def _():
            img_add(it - reach)

        for g in range(GROUPS):
            done = reach + (g + 1) * chunks - 1

            @pl.when(it == done)
            def _():
                scatter_across(img_mine, img_rs, g)

            if g < GROUPS - 1:
                @pl.when(it == done + 2)
                def _():
                    scatter_between(img_mine, img_rs, g)

    images = [scatter_end(img_mine, img_rs, g) for g in range(GROUPS - 1)]
    scatter_between(img_mine, img_rs, GROUPS - 1)
    images.append(scatter_end(img_mine, img_rs, GROUPS - 1))
    image = jnp.concatenate(images, axis=0).T
    image = image + ridge_weight * dir_ref[...]
    image_ref[...] = image

    def rows_sum(value):
        return jnp.sum(value, axis=0, keepdims=True)

    inputs[3].wait()
    residual = res_ref[...]
    sc_own[...] = jnp.concatenate(
        [
            rows_sum(residual * residual),
            rows_sum(dir_ref[...] * image),
            rows_sum(residual * image),
            rows_sum(image * image),
            jnp.zeros((4, OUTS), F32),
        ],
        axis=0,
    )

    def cent_copy(d):
        return pltpu.make_async_remote_copy(
            src_ref=sc_own, dst_ref=sc_cent.at[d],
            send_sem=sc_sems.at[0, d], recv_sem=sc_sems.at[1, d],
            device_id=(z, lax.rem(me + d, cent_n)), device_id_type=MESH,
        )

    def rows_copy(d):
        return pltpu.make_async_remote_copy(
            src_ref=sc_mid, dst_ref=sc_rows.at[d],
            send_sem=sc_sems.at[2, d], recv_sem=sc_sems.at[3, d],
            device_id=(lax.rem(z + d, rows_n), me), device_id_type=MESH,
        )

    for d in range(1, cent_n):
        cent_copy(d).start()
    total = sc_own[...]
    for d in range(1, cent_n):
        cent_copy(d).wait_recv()
        total = total + sc_cent[d]
    sc_mid[...] = total
    for d in range(1, rows_n):
        rows_copy(d).start()
    gather_sent(0, dir_own, dir_all)
    for g in range(GROUPS):
        gather_sent(1 + g, fit_own.at[g], fit_all.at[g])
    scatter_sent(fit_rs)
    scatter_sent(img_rs)
    scan_sent(pick)
    scan_sent(coef)
    scan_sent(grad)
    for d in range(1, cent_n):
        cent_copy(d).wait_send()
    for d in range(1, rows_n):
        rows_copy(d).wait_recv()
        total = total + sc_rows[d]
    sums_ref[...] = total
    for d in range(1, rows_n):
        rows_copy(d).wait_send()


def update_kernel(sums_ref, image_ref, coef_ref, res_ref, dir_ref, coef_out, res_out, dir_out):
    totals = jnp.sum(sums_ref[...], axis=1, keepdims=True)
    norm_old, curvature, cross, square = (totals[at : at + 1] for at in range(4))
    step_size = norm_old / curvature
    norm_new = norm_old - 2.0 * step_size * cross + step_size * step_size * square
    ratio = norm_new / norm_old
    direction = dir_ref[...]
    coef_out[...] = coef_ref[...] + step_size * direction
    residual_next = res_ref[...] - step_size * image_ref[...]
    res_out[...] = residual_next
    dir_out[...] = residual_next + ratio * direction


def on_device(rows_n, cent_n, train_rows, centre_index, precond, coefficients, residual, direction):
    rows_here = train_rows.shape[0]
    centres_here = centre_index.shape[0]
    part = direction.shape[0]
    chunks = centres_here // CHUNK
    chips = cent_n // 2
    fit_part = rows_here // cent_n
    group = OUTS // GROUPS
    vmem = pl.BlockSpec(memory_space=pltpu.VMEM)

    def scan(count, shape, own_dtype, link_dtype):
        piece = (count,) + shape
        return (
            pltpu.VMEM(piece, own_dtype),
            pltpu.VMEM(piece, link_dtype), pltpu.VMEM(piece, link_dtype),
            pltpu.VMEM(piece, link_dtype), pltpu.VMEM(piece, link_dtype),
            pltpu.SemaphoreType.DMA((4, count)),
        )

    def scatter(shape):
        piece = (GROUPS, chips) + shape
        return (
            pltpu.VMEM(piece, BF16), pltpu.VMEM(piece, BF16),
            pltpu.VMEM(piece, BF16), pltpu.VMEM(piece, BF16),
            pltpu.SemaphoreType.DMA((GROUPS, 4, chips)),
        )

    image, sums = pl.pallas_call(
        functools.partial(step_kernel, rows_n, cent_n),
        out_shape=(
            jax.ShapeDtypeStruct((part, OUTS), F32),
            jax.ShapeDtypeStruct((8, OUTS), F32),
        ),
        in_specs=[pl.BlockSpec(memory_space=pl.ANY)] * 5,
        out_specs=(vmem, vmem),
        scratch_shapes=[
            pltpu.VMEM((chunks, 1, CHUNK), I32),
            pltpu.VMEM((FEAT, rows_here), F32),
            pltpu.VMEM((part, OUTS), F32),
            pltpu.VMEM((part, OUTS), F32),
            pltpu.SemaphoreType.DMA((4,)),
            pltpu.VMEM((chunks, CHUNK, precond.shape[1]), BF16),
            pltpu.SemaphoreType.DMA((chunks,)),
            pltpu.VMEM((chunks, rows_here // CHUNK, CHUNK, CHUNK), BF16),
            pltpu.VMEM((rows_here, 4 * FEAT), BF16),
            pltpu.VMEM((4 * FEAT, rows_here), BF16),
            pltpu.VMEM((chunks, 4 * FEAT, CHUNK), BF16),
            pltpu.VMEM((2 * FEAT, rows_here), BF16),
            scan(chunks, (FEAT, CHUNK), I16, I16),
            scan(GROUPS * chunks, (group, CHUNK), F32, BF16),
            scan(GROUPS * chunks, (group, CHUNK), F32, BF16),
            pltpu.VMEM((OUTS, part), BF16),
            pltpu.VMEM((cent_n, OUTS, part), BF16),
            pltpu.VMEM((GROUPS, group, fit_part), BF16),
            pltpu.VMEM((GROUPS, cent_n, group, fit_part), BF16),
            pltpu.SemaphoreType.DMA((1 + GROUPS, 4, chips)),
            pltpu.VMEM((cent_n, OUTS, fit_part), F32),
            scatter((group, fit_part)),
            pltpu.VMEM((GROUPS, cent_n, group, part), F32),
            scatter((group, part)),
            pltpu.VMEM((8, OUTS), F32),
            pltpu.VMEM((cent_n, 8, OUTS), F32),
            pltpu.VMEM((8, OUTS), F32),
            pltpu.VMEM((rows_n, 8, OUTS), F32),
            pltpu.SemaphoreType.DMA((4, max(cent_n, rows_n))),
        ],
        compiler_params=pltpu.CompilerParams(
            collective_id=0, has_side_effects=True, vmem_limit_bytes=67000000
        ),
        name="falkon_step",
    )(centre_index.reshape(chunks, 1, CHUNK), train_rows.T, precond, residual, direction)

    piece = jax.ShapeDtypeStruct((part, OUTS), F32)
    return pl.pallas_call(
        update_kernel,
        out_shape=(piece, piece, piece),
        in_specs=[vmem] * 5,
        out_specs=(vmem, vmem, vmem),
        name="falkon_update",
    )(sums, image, coefficients, residual, direction)


def solution(mesh):
    both = P(("rows", "cent"), None)
    return jax.shard_map(
        functools.partial(on_device, mesh.shape["rows"], mesh.shape["cent"]),
        mesh=mesh,
        in_specs=(P("rows", None), P("cent"), P("cent", "rows"), both, both, both),
        out_specs=(both, both, both),
        check_vma=False,
    )
```

```python
import functools
import math

import jax
import jax.numpy as jnp
from jax import lax
from jax.experimental import pallas as pl
from jax.experimental.pallas import tpu as pltpu
from jax.sharding import PartitionSpec as P

FEAT = 64
OUTS = 128
CHUNK = 256
GROUPS = 2
LAG = 5
CUTS = (1, 5, 7)
NEAR_AT = 8
NEAR_SLOTS = 4
FORWARD_BEFORE = 2
COEF_AT = 12
BUILD_AFTER = 0
WIDEST = 6.0
F32 = jnp.float32
BF16 = jnp.bfloat16
I16 = jnp.int16
I32 = jnp.int32
MESH = pl.DeviceIdType.MESH
STEPS = 5461.0
LOG2E = math.log2(math.e)
CROSS = LOG2E * 4.0 / FEAT / STEPS
POINT_NORM = -STEPS * STEPS * FEAT / (8.0 * LOG2E)
CENTRE_NORM = -LOG2E * 2.0 / FEAT / (STEPS * STEPS)

ridge_weight = 0.1


def dot(a, b):
    return jnp.dot(a, b, preferred_element_type=F32)


def dot_t(a, b):
    return lax.dot_general(a, b, (((1,), (1,)), ((), ())), preferred_element_type=F32)


def three(value):
    high = value.astype(BF16)
    rest = value - high.astype(F32)
    middle = rest.astype(BF16)
    low = (rest - middle.astype(F32)).astype(BF16)
    return high.astype(F32), middle.astype(F32), low.astype(F32)


def augmented(high, low, norm_scale, norm_at, one_at):
    exact = high + low
    norm = norm_scale * jnp.sum(exact * exact, axis=0, keepdims=True)
    sub = lax.broadcasted_iota(I32, high.shape, 0)
    extra = jnp.where((sub >= one_at) & (sub < one_at + 3), 1.0, 0.0)
    for at, term in enumerate(three(norm)):
        extra = jnp.where(sub == norm_at + at, term, extra)
    return extra


def step_kernel(
    rows_n, cent_n,
    idx_hbm, x_hbm, p_hbm, res_hbm, dir_hbm,
    image_ref, sums_ref,
    idx_ref, x_ref, res_ref, dir_ref, in_sems,
    p_buf, p_sem, k_buf, xaug, xaug_t, caug_t, nhl_t,
    pick, coef, grad,
    dir_own, dir_all, fit_own, fit_all, gather_sems,
    fit_acc, fit_rs, img_acc, img_rs,
    sc_own, sc_cent, sc_mid, sc_rows, sc_sems,
):
    z = lax.axis_index("rows")
    me = lax.axis_index("cent")
    core = lax.rem(me, 2)
    chip = lax.div(me, 2)
    other = chip * 2 + (1 - core)
    chips = cent_n // 2
    chunks = p_buf.shape[0]
    rows_here = x_ref.shape[1]
    part = dir_own.shape[1]
    fit_part = fit_acc.shape[2]
    group = OUTS // GROUPS
    items = GROUPS * chunks
    last = rows_n - 1
    reach = LAG * last

    near = chips - 1
    paired = chips & (chips - 1) == 0

    def chip_at(distance):
        if not paired:
            return lax.rem(chip + distance, chips)
        at = chip
        bit = 1
        while bit < chips:
            if distance & bit:
                at = at + bit * (1 - 2 * lax.rem(lax.div(at, bit), 2))
            bit *= 2
        return at

    def chip_from(distance):
        return chip_at(distance) if paired else chip_at(chips - distance)

    def p_copy(k):
        return pltpu.make_async_copy(
            p_hbm.at[pl.ds(pl.multiple_of(k * CHUNK, CHUNK), CHUNK)], p_buf.at[k], p_sem.at[k]
        )

    barrier = pltpu.get_barrier_semaphore()
    for d in range(1, cent_n):
        pl.semaphore_signal(
            barrier, inc=1, device_id=(z, lax.rem(me + d, cent_n)), device_id_type=MESH
        )
    for d in range(1, rows_n):
        pl.semaphore_signal(
            barrier, inc=1, device_id=(lax.rem(z + d, rows_n), me), device_id_type=MESH
        )

    inputs = [
        pltpu.make_async_copy(source, target, in_sems.at[at])
        for at, (source, target) in enumerate(
            ((dir_hbm, dir_ref), (x_hbm, x_ref), (idx_hbm, idx_ref), (res_hbm, res_ref))
        )
    ]
    for copy in inputs:
        copy.start()

    @pl.loop(0, chunks)
    def _(k):
        p_copy(k).start()

    inputs[0].wait()
    dir_own[...] = dir_ref[...].T.astype(BF16)
    for scan in (pick, coef, grad):
        @pl.when(z == 0)
        def _():
            scan[3][...] = jnp.zeros_like(scan[3])

        @pl.when(z == last)
        def _():
            scan[4][...] = jnp.zeros_like(scan[4])

    pl.semaphore_wait(barrier, cent_n - 1 + rows_n - 1)

    def gather_copy(which, own, whole, d):
        target = other if d == 0 else chip_at(d) * 2 + core
        return pltpu.make_async_remote_copy(
            src_ref=own, dst_ref=whole.at[me],
            send_sem=gather_sems.at[which, 0, d], recv_sem=gather_sems.at[which, 1, d],
            device_id=(z, target), device_id_type=MESH,
        )

    def forward_copy(which, whole, d):
        source = chip_from(d) * 2 + core
        return pltpu.make_async_remote_copy(
            src_ref=whole.at[source], dst_ref=whole.at[source],
            send_sem=gather_sems.at[which, 2, d], recv_sem=gather_sems.at[which, 3, d],
            device_id=(z, other), device_id_type=MESH,
        )

    def gather_start(which, own, whole):
        order = range(1, chips) if which == 0 else range(chips - 1, 0, -1)
        for d in [*order, 0]:
            gather_copy(which, own, whole, d).start()
        whole[me] = own[...]

    def gather_forward(which, own, whole, distances):
        for d in distances:
            gather_copy(which, own, whole, d).wait_recv()
            forward_copy(which, whole, d).start()

    def gather_end(which, own, whole, distances):
        for d in distances:
            if d == 0:
                gather_copy(which, own, whole, 0).wait_recv()
            else:
                forward_copy(which, whole, d).wait_recv()

    def gather_sent(which, own, whole):
        for d in range(chips):
            gather_copy(which, own, whole, d).wait_send()
        for d in range(1, chips):
            forward_copy(which, whole, d).wait_send()

    def right_copy(scan, k):
        own, to_right, to_left, from_left, from_right, sems = scan
        return pltpu.make_async_remote_copy(
            src_ref=to_right.at[k], dst_ref=from_left.at[k],
            send_sem=sems.at[0, k], recv_sem=sems.at[1, k],
            device_id=(lax.rem(z + 1, rows_n), me), device_id_type=MESH,
        )

    def left_copy(scan, k):
        own, to_right, to_left, from_left, from_right, sems = scan
        return pltpu.make_async_remote_copy(
            src_ref=to_left.at[k], dst_ref=from_right.at[k],
            send_sem=sems.at[2, k], recv_sem=sems.at[3, k],
            device_id=(lax.rem(z + last, rows_n), me), device_id_type=MESH,
        )

    def wide(scan):
        return I32 if scan[0].dtype == I16 else F32

    def scan_step(scan, it):
        own, to_right, to_left, from_left, from_right, sems = scan
        kr = it - LAG * z
        kl = it - LAG * (last - z)
        kind = wide(scan)

        @pl.when((kr >= 0) & (kr < own.shape[0]) & (z < last))
        def _():
            @pl.when(z > 0)
            def _():
                right_copy(scan, kr).wait_recv()

            to_right[kr] = (own[kr].astype(kind) + from_left[kr].astype(kind)).astype(to_right.dtype)
            right_copy(scan, kr).start()

        @pl.when((kl >= 0) & (kl < own.shape[0]) & (z > 0))
        def _():
            @pl.when(z < last)
            def _():
                left_copy(scan, kl).wait_recv()

            to_left[kl] = (own[kl].astype(kind) + from_right[kl].astype(kind)).astype(to_left.dtype)
            left_copy(scan, kl).start()

    def scan_total(scan, k):
        own, to_right, to_left, from_left, from_right, sems = scan
        kind = wide(scan)

        @pl.when(z == last)
        def _():
            right_copy(scan, k).wait_recv()

        @pl.when(z == 0)
        def _():
            left_copy(scan, k).wait_recv()

        return own[k].astype(kind) + from_left[k].astype(kind) + from_right[k].astype(kind)

    def scan_sent(scan):
        @pl.loop(0, scan[0].shape[0])
        def _(k):
            @pl.when(z < last)
            def _():
                right_copy(scan, k).wait_send()

            @pl.when(z > 0)
            def _():
                left_copy(scan, k).wait_send()

    def across_copy(buffers, g, q):
        send_a, recv_a, send_b, recv_b, sems = buffers
        return pltpu.make_async_remote_copy(
            src_ref=send_a.at[g, q], dst_ref=recv_a.at[g, q],
            send_sem=sems.at[g, 0, q], recv_sem=sems.at[g, 1, q],
            device_id=(z, other), device_id_type=MESH,
        )

    def between_copy(buffers, g, d):
        send_a, recv_a, send_b, recv_b, sems = buffers
        return pltpu.make_async_remote_copy(
            src_ref=send_b.at[g, d], dst_ref=recv_b.at[g, d],
            send_sem=sems.at[g, 2, d], recv_sem=sems.at[g, 3, d],
            device_id=(z, chip_at(d) * 2 + core), device_id_type=MESH,
        )

    def scatter_across(mine, buffers, g):
        for d in list(range(chips - 1, 0, -1)) + [0]:
            q = chip_at(d)
            buffers[0][g, q] = mine(g, q * 2 + (1 - core)).astype(BF16)
            across_copy(buffers, g, q).start()

    def scatter_between(mine, buffers, g):
        send_a, recv_a, send_b, recv_b, sems = buffers
        for d in range(chips - 1, 0, -1):
            q = chip_at(d)
            across_copy(buffers, g, q).wait_recv()
            send_b[g, d] = (mine(g, q * 2 + core) + recv_a[g, q].astype(F32)).astype(BF16)
            between_copy(buffers, g, d).start()

    def scatter_end(mine, buffers, g):
        send_a, recv_a, send_b, recv_b, sems = buffers
        across_copy(buffers, g, chip).wait_recv()
        total = mine(g, me) + recv_a[g, chip].astype(F32)
        for d in range(1, chips):
            between_copy(buffers, g, d).wait_recv()
            total = total + recv_b[g, d].astype(F32)
        return total

    def scatter_sent(buffers):
        for g in range(GROUPS):
            for d in range(chips):
                across_copy(buffers, g, chip_at(d)).wait_send()
            for d in range(1, chips):
                between_copy(buffers, g, d).wait_send()

    gather_start(0, dir_own, dir_all)
    inputs[1].wait()
    inputs[2].wait()
    closer, farthest, every = range(1, near), range(near, chips), range(chips)

    x_block = rows_here // chunks
    for b in range(chunks):
        here = slice(b * x_block, (b + 1) * x_block)
        number = jnp.round(x_ref[:, here] * STEPS)
        high = number.astype(BF16)
        nhl_t[:FEAT, here] = high
        nhl_t[FEAT:, here] = (number - high.astype(F32)).astype(BF16)

    def augment_points(b):
        here = pl.ds(pl.multiple_of(b * x_block, x_block), x_block)
        points = x_ref[:, here] * CROSS
        high = points.astype(BF16).astype(F32)
        low = (points - high).astype(BF16).astype(F32)
        extra = augmented(high, low, POINT_NORM, 0, 3)
        for at, term in enumerate((high, low, high, extra)):
            xaug_t[at * FEAT : (at + 1) * FEAT, here] = term.astype(BF16)
        xaug[here, :] = jnp.concatenate([high, low, high, extra], axis=0).T.astype(BF16)

    pick_block = math.gcd(rows_here, 1024)

    def pick_own(k):
        wanted = idx_ref[k] - z * rows_here
        total = jnp.zeros((2 * FEAT, CHUNK), F32)
        for b in range(rows_here // pick_block):
            ids = lax.broadcasted_iota(I32, (pick_block, CHUNK), 0) + b * pick_block
            hot = jnp.where(ids == wanted, 1.0, 0.0).astype(BF16)
            total = total + dot(nhl_t[:, b * pick_block : (b + 1) * pick_block], hot)
        pick[0][k] = (total[:FEAT] + total[FEAT:]).astype(I32).astype(I16)

    def coef_blocks(k, blocks):
        total = jnp.zeros((OUTS, CHUNK), F32)
        for block in blocks:
            here = pl.ds(pl.multiple_of(block * part, part), part)
            total = total + dot_t(dir_all[block], p_buf[k, :, here])
        return total

    def pair(d):
        return [chip_from(d) * 2 + core, chip_from(d) * 2 + 1 - core]

    def coef_near(k):
        p_copy(k).wait()
        total = coef_blocks(k, [me, other] + [b for d in closer for b in pair(d)])
        for g in range(GROUPS):
            coef[0][k * GROUPS + g] = total[g * group : (g + 1) * group]

    def coef_far(k):
        total = coef_blocks(k, [b for d in farthest for b in pair(d)])
        for g in range(GROUPS):
            coef[0][k * GROUPS + g] += total[g * group : (g + 1) * group]

    fit_blocks = fit_part // CHUNK

    def build(k):
        number = scan_total(pick, k).astype(F32)
        high = number.astype(BF16).astype(F32)
        low = number - high
        extra = augmented(high, low, CENTRE_NORM, 3, 0)
        caug = jnp.concatenate([high, high, low, extra], axis=0)
        caug_t[k] = caug.astype(BF16)
        caug = caug.T.astype(BF16)
        for b in range(rows_here // CHUNK):
            here = slice(b * CHUNK, (b + 1) * CHUNK)
            k_buf[k, b] = jnp.exp2(dot(caug, xaug_t[:, here])).astype(BF16)

    def rebuild(k):
        for b in range(rows_here // CHUNK):
            here = slice(b * CHUNK, (b + 1) * CHUNK)
            k_buf[k, b] = jnp.exp2(dot(xaug[here, :], caug_t[k])).astype(BF16)

    def fit_add(k):
        low = jnp.concatenate(
            [scan_total(coef, k * GROUPS + g).astype(BF16) for g in range(GROUPS)], axis=0
        )
        for b in range(cent_n):
            for h in range(fit_blocks):
                here = slice(h * CHUNK, (h + 1) * CHUNK)
                fit_acc[b, :, here] += dot(low, k_buf[k, b * fit_blocks + h])

    def fit_mine(g, block):
        return fit_acc[block, g * group : (g + 1) * group, :]

    def img_mine(g, block):
        return img_acc[g, block]

    fit_acc[...] = jnp.zeros_like(fit_acc)
    img_acc[...] = jnp.zeros_like(img_acc)
    build_at = max(COEF_AT + BUILD_AFTER, LAG * (last - 1))
    fit_at = COEF_AT + reach

    def turn(it, start, phase):
        step = it - start
        return (step >= 0) & (step < items) & (lax.rem(step + items, GROUPS) == phase)

    @pl.loop(0, fit_at + items)
    def _(it):
        @pl.when(it < chunks)
        def _():
            pick_own(it)

        scan_step(pick, it)

        @pl.when(it < chunks)
        def _():
            augment_points(it)

        for at, distances in ((NEAR_AT, closer), (COEF_AT, farthest)):
            @pl.when(it == at - FORWARD_BEFORE)
            def _():
                gather_forward(0, dir_own, dir_all, distances)

            @pl.when(it == at)
            def _():
                if at == NEAR_AT:
                    gather_end(0, dir_own, dir_all, [0])
                gather_end(0, dir_own, dir_all, distances)

        @pl.when((it >= NEAR_AT) & (it < NEAR_AT + NEAR_SLOTS))
        def _():
            @pl.loop(0, chunks // NEAR_SLOTS)
            def _(step):
                coef_near((it - NEAR_AT) * (chunks // NEAR_SLOTS) + step)

        @pl.when(turn(it, COEF_AT, 0))
        def _():
            coef_far(lax.div(it - COEF_AT, GROUPS))

        scan_step(coef, it - COEF_AT)

        @pl.when(turn(it, build_at, GROUPS - 1))
        def _():
            build(lax.div(it - build_at, GROUPS))

        @pl.when(turn(it, fit_at, GROUPS - 1))
        def _():
            fit_add(lax.div(it - fit_at, GROUPS))

    def fit_shared(g):
        fit_own[g] = scatter_end(fit_mine, fit_rs, g).astype(BF16)
        gather_start(1 + g, fit_own.at[g], fit_all.at[g])

    def rebuild_some(start, stop):
        @pl.loop(start, stop)
        def _(k):
            rebuild(k)

    cuts = [chunks * c // 8 for c in CUTS]
    for g in range(GROUPS):
        scatter_across(fit_mine, fit_rs, g)
    rebuild_some(0, cuts[0])
    for g in range(GROUPS):
        scatter_between(fit_mine, fit_rs, g)
    rebuild_some(cuts[0], cuts[1])
    fit_shared(0)
    rebuild_some(cuts[1], cuts[2])
    for g in range(1, GROUPS):
        fit_shared(g)
    rebuild_some(cuts[2], chunks)
    gather_forward(1, fit_own.at[0], fit_all.at[0], range(1, chips))
    gather_end(1, fit_own.at[0], fit_all.at[0], every)

    scale = float(rows_here * rows_n) ** -0.5

    def grad_own(i):
        g = lax.div(i, chunks)
        k = lax.rem(i, chunks)
        total = jnp.zeros((group, CHUNK), F32)
        for b in range(cent_n):
            for h in range(fit_blocks):
                here = slice(h * CHUNK, (h + 1) * CHUNK)
                total = total + dot(fit_all[g, b, :, here], k_buf[k, b * fit_blocks + h])
        grad[0][i] = total

    def img_add(i):
        g = lax.div(i, chunks)
        k = lax.rem(i, chunks)
        low = (scan_total(grad, i) * scale).astype(BF16)
        for b in range(cent_n):
            img_acc[g, b] += dot(low, p_buf[k, :, b * part : (b + 1) * part])

    @pl.loop(0, items + reach)
    def _(it):
        @pl.when(it == (GROUPS - 1) * chunks - FORWARD_BEFORE)
        def _():
            g = GROUPS - 1
            gather_forward(1 + g, fit_own.at[g], fit_all.at[g], range(1, chips))

        for g in range(1, GROUPS):
            @pl.when(it == g * chunks)
            def _():
                gather_end(1 + g, fit_own.at[g], fit_all.at[g], every)

        @pl.when(it < items)
        def _():
            grad_own(it)

        scan_step(grad, it)

        @pl.when(it >= reach)
        def _():
            img_add(it - reach)

        for g in range(GROUPS):
            done = reach + (g + 1) * chunks - 1

            @pl.when(it == done)
            def _():
                scatter_across(img_mine, img_rs, g)

            if g < GROUPS - 1:
                @pl.when(it == done + 2)
                def _():
                    scatter_between(img_mine, img_rs, g)

    images = [scatter_end(img_mine, img_rs, g) for g in range(GROUPS - 1)]
    scatter_between(img_mine, img_rs, GROUPS - 1)
    images.append(scatter_end(img_mine, img_rs, GROUPS - 1))
    image = jnp.concatenate(images, axis=0).T
    image = image + ridge_weight * dir_ref[...]
    image_ref[...] = image

    def rows_sum(value):
        return jnp.sum(value, axis=0, keepdims=True)

    inputs[3].wait()
    residual = res_ref[...]
    sc_own[...] = jnp.concatenate(
        [
            rows_sum(residual * residual),
            rows_sum(dir_ref[...] * image),
            rows_sum(residual * image),
            rows_sum(image * image),
            jnp.zeros((4, OUTS), F32),
        ],
        axis=0,
    )

    def cent_copy(d):
        return pltpu.make_async_remote_copy(
            src_ref=sc_own, dst_ref=sc_cent.at[d],
            send_sem=sc_sems.at[0, d], recv_sem=sc_sems.at[1, d],
            device_id=(z, lax.rem(me + d, cent_n)), device_id_type=MESH,
        )

    def rows_copy(d):
        return pltpu.make_async_remote_copy(
            src_ref=sc_mid, dst_ref=sc_rows.at[d],
            send_sem=sc_sems.at[2, d], recv_sem=sc_sems.at[3, d],
            device_id=(lax.rem(z + d, rows_n), me), device_id_type=MESH,
        )

    for d in range(1, cent_n):
        cent_copy(d).start()
    total = sc_own[...]
    for d in range(1, cent_n):
        cent_copy(d).wait_recv()
        total = total + sc_cent[d]
    sc_mid[...] = total
    for d in range(1, rows_n):
        rows_copy(d).start()
    gather_sent(0, dir_own, dir_all)
    for g in range(GROUPS):
        gather_sent(1 + g, fit_own.at[g], fit_all.at[g])
    scatter_sent(fit_rs)
    scatter_sent(img_rs)
    scan_sent(pick)
    scan_sent(coef)
    scan_sent(grad)
    for d in range(1, cent_n):
        cent_copy(d).wait_send()
    for d in range(1, rows_n):
        rows_copy(d).wait_recv()
        total = total + sc_rows[d]
    sums_ref[...] = total
    for d in range(1, rows_n):
        rows_copy(d).wait_send()


def update_kernel(sums_ref, image_ref, coef_ref, res_ref, dir_ref, coef_out, res_out, dir_out):
    totals = jnp.sum(sums_ref[...], axis=1, keepdims=True)
    norm_old, curvature, cross, square = (totals[at : at + 1] for at in range(4))
    step_size = norm_old / curvature
    norm_new = norm_old - 2.0 * step_size * cross + step_size * step_size * square
    ratio = norm_new / norm_old
    direction = dir_ref[...]
    coef_out[...] = coef_ref[...] + step_size * direction
    residual_next = res_ref[...] - step_size * image_ref[...]
    res_out[...] = residual_next
    dir_out[...] = residual_next + ratio * direction


def on_device(rows_n, cent_n, train_rows, centre_index, precond, coefficients, residual, direction):
    rows_here = train_rows.shape[0]
    centres_here = centre_index.shape[0]
    part = direction.shape[0]
    chunks = centres_here // CHUNK
    chips = cent_n // 2
    fit_part = rows_here // cent_n
    group = OUTS // GROUPS
    vmem = pl.BlockSpec(memory_space=pltpu.VMEM)

    def scan(count, shape, own_dtype, link_dtype):
        piece = (count,) + shape
        return (
            pltpu.VMEM(piece, own_dtype),
            pltpu.VMEM(piece, link_dtype), pltpu.VMEM(piece, link_dtype),
            pltpu.VMEM(piece, link_dtype), pltpu.VMEM(piece, link_dtype),
            pltpu.SemaphoreType.DMA((4, count)),
        )

    def scatter(shape):
        piece = (GROUPS, chips) + shape
        return (
            pltpu.VMEM(piece, BF16), pltpu.VMEM(piece, BF16),
            pltpu.VMEM(piece, BF16), pltpu.VMEM(piece, BF16),
            pltpu.SemaphoreType.DMA((GROUPS, 4, chips)),
        )

    image, sums = pl.pallas_call(
        functools.partial(step_kernel, rows_n, cent_n),
        out_shape=(
            jax.ShapeDtypeStruct((part, OUTS), F32),
            jax.ShapeDtypeStruct((8, OUTS), F32),
        ),
        in_specs=[pl.BlockSpec(memory_space=pl.ANY)] * 5,
        out_specs=(vmem, vmem),
        scratch_shapes=[
            pltpu.VMEM((chunks, 1, CHUNK), I32),
            pltpu.VMEM((FEAT, rows_here), F32),
            pltpu.VMEM((part, OUTS), F32),
            pltpu.VMEM((part, OUTS), F32),
            pltpu.SemaphoreType.DMA((4,)),
            pltpu.VMEM((chunks, CHUNK, precond.shape[1]), BF16),
            pltpu.SemaphoreType.DMA((chunks,)),
            pltpu.VMEM((chunks, rows_here // CHUNK, CHUNK, CHUNK), BF16),
            pltpu.VMEM((rows_here, 4 * FEAT), BF16),
            pltpu.VMEM((4 * FEAT, rows_here), BF16),
            pltpu.VMEM((chunks, 4 * FEAT, CHUNK), BF16),
            pltpu.VMEM((2 * FEAT, rows_here), BF16),
            scan(chunks, (FEAT, CHUNK), I16, I16),
            scan(GROUPS * chunks, (group, CHUNK), F32, BF16),
            scan(GROUPS * chunks, (group, CHUNK), F32, BF16),
            pltpu.VMEM((OUTS, part), BF16),
            pltpu.VMEM((cent_n, OUTS, part), BF16),
            pltpu.VMEM((GROUPS, group, fit_part), BF16),
            pltpu.VMEM((GROUPS, cent_n, group, fit_part), BF16),
            pltpu.SemaphoreType.DMA((1 + GROUPS, 4, chips)),
            pltpu.VMEM((cent_n, OUTS, fit_part), F32),
            scatter((group, fit_part)),
            pltpu.VMEM((GROUPS, cent_n, group, part), F32),
            scatter((group, part)),
            pltpu.VMEM((8, OUTS), F32),
            pltpu.VMEM((cent_n, 8, OUTS), F32),
            pltpu.VMEM((8, OUTS), F32),
            pltpu.VMEM((rows_n, 8, OUTS), F32),
            pltpu.SemaphoreType.DMA((4, max(cent_n, rows_n))),
        ],
        compiler_params=pltpu.CompilerParams(
            collective_id=0, has_side_effects=True, vmem_limit_bytes=67000000
        ),
        name="falkon_step",
    )(centre_index.reshape(chunks, 1, CHUNK), train_rows.T, precond, residual, direction)

    piece = jax.ShapeDtypeStruct((part, OUTS), F32)
    return pl.pallas_call(
        update_kernel,
        out_shape=(piece, piece, piece),
        in_specs=[vmem] * 5,
        out_specs=(vmem, vmem, vmem),
        name="falkon_update",
    )(sums, image, coefficients, residual, direction)


def solution(mesh):
    both = P(("rows", "cent"), None)
    return jax.shard_map(
        functools.partial(on_device, mesh.shape["rows"], mesh.shape["cent"]),
        mesh=mesh,
        in_specs=(P("rows", None), P("cent"), P("cent", "rows"), both, both, both),
        out_specs=(both, both, both),
        check_vma=False,
    )
```
